32 devices in a mesh: dp: 8 (over z, y), tensor: 4 (over x, core).
Axes of the slice: x: 2, y: 2, z: 4, core: 2. Of those that a mesh axis runs over, the one named last changes fastest.
Arguments:
- block_in: bfloat16 [8192, 768], P(('dp', 'tensor')), may hold values from -81 to 81
- seq_lengths: int32 [8, 1], P('dp'), may hold values from 1 to 1024, as said below
- attn_gain: bfloat16 [768], P('dp'), may hold values from 0.25 to 1.75
- qkv_weight: bfloat16 [768, 2304], P('dp', 'tensor'), may hold values from -4 to 4
- out_weight: bfloat16 [768, 768], P('tensor', 'dp'), may hold values from -1.25 to 1.25
- mlp_gain: bfloat16 [768], P('dp'), may hold values from 0.25 to 1.75
- act_weight: bfloat16 [768, 1152], P('dp', 'tensor'), may hold values from -0.21875 to 0.21875
- gate_weight: bfloat16 [768, 1152], P('dp', 'tensor'), may hold values from -0.21875 to 0.21875
- down_weight: bfloat16 [1152, 768], P('tensor', 'dp'), may hold values from -0.375 to 0.375
- block_cot: bfloat16 [8192, 768], P(('dp', 'tensor')), may hold values from -12 to 12
Outputs:
- block_out: bfloat16 [8192, 768], P(('dp', 'tensor'))
- input_grad: float32 [8192, 768], P(('dp', 'tensor'))
- attn_gain_grad: float32 [768], P('dp')
- qkv_grad: float32 [768, 2304], P('dp', 'tensor')
- out_grad: float32 [768, 768], P('tensor', 'dp')
- mlp_gain_grad: float32 [768], P('dp')
- act_grad: float32 [768, 1152], P('dp', 'tensor')
- gate_grad: float32 [768, 1152], P('dp', 'tensor')
- down_grad: float32 [1152, 768], P('tensor', 'dp')
The draws below stay inside these ranges and needn't reach their ends.
Inputs may be any that keep to these rules, and one draw needn't show every extreme that they name: `seq_lengths`: row g holds the lengths of the 1 sequence of index g of dp, in the order in which they lie in its 1024 token slots from the first; the slots after them are padding. In every draw some row has all its lengths equal to 1024.
All inputs are finite; a program needn't handle non-finite values.
Results may differ from the reference program's by a relative error of at most 0.02.
The reference program's roundings to bfloat16 on the way count: a program that leaves them out, or rounds other values in their place, can miss the bound.
Values may be sent and summed in bfloat16 or wider, within the bound.
No kernel may reach another device: no remote copies, remote signals or barrier semaphores. Data moves between devices by JAX's collectives and lax.ppermute only.
A program may use at most 128 MiB of HBM per device.

```python
import jax
import jax.numpy as jnp
from jax import lax

D = 768
HEADS = 12
HD = 64
FF = 1152
HALF = 64
SLOTS = 1
TOK_DEV = 1024
LMAX = 1024
BLOCK = 512
TOKENS = 8192
N_DP = 8
N_TENSOR = 4


def draw_block_in(key, part):
    noise_key, row_key, col_key = jax.random.split(key, 3)
    row_scale = jnp.exp(jax.random.uniform(row_key, (TOKENS, 1), minval=0.0, maxval=jnp.log(10.0)))
    col_scale = jnp.exp(jax.random.uniform(col_key, (1, D), minval=-0.69, maxval=0.69))
    base = jnp.clip(jax.random.normal(noise_key, (TOKENS, D)), -4.0, 4.0)
    return (base * row_scale * col_scale).astype(jnp.bfloat16)


def draw_seq_lengths(key, part):
    length_key, row_key = jax.random.split(key)
    lengths = jax.random.randint(length_key, (N_DP, SLOTS), 1, LMAX + 1)
    full_row = jax.random.randint(row_key, (), 0, N_DP)
    return jnp.where(jnp.arange(N_DP)[:, None] == full_row, LMAX, lengths).astype(jnp.int32)


def draw_qkv_weight(key, part):
    noise_key = jax.random.fold_in(key, 0)
    noise = jnp.clip(jax.random.normal(noise_key, (D, HEADS, 3, HD)), -4.0, 4.0)
    mixed = noise
    return (mixed / jnp.sqrt(D * 1.0)).reshape(D, 3 * D).astype(jnp.bfloat16)


def draw_block_cot(key, part):
    noise_key = jax.random.fold_in(key, 0)
    rising = 1.0 + 2.0 * jnp.arange(TOKENS, dtype=jnp.float32)[:, None] / TOKENS
    base = jnp.clip(jax.random.normal(noise_key, (TOKENS, D)), -4.0, 4.0)
    return (base * rising).astype(jnp.bfloat16)


def level_of(key, shape, pieces, low, top_value):
    def one(dim, shards_of):
        draws = jax.random.uniform(jax.random.fold_in(jax.random.fold_in(key, 6), dim), (shards_of,), jnp.float32, low / len(pieces), top_value / len(pieces))
        return jnp.repeat(jnp.exp(draws), shape[dim] // shards_of).reshape((-1,) + (1,) * (len(shape) - dim - 1))

    factor_of = one(*pieces[0])
    for cut in pieces[1:]:
        factor_of = factor_of * one(*cut)
    return factor_of


def scatter_about(own_key, extent, scale, most, cuts=(), kind=jnp.bfloat16):
    drawn = scale * jax.random.normal(own_key, extent, jnp.float32)
    if cuts:
        drawn = drawn * level_of(own_key, extent, cuts, -0.22, 0.18)
    return jnp.clip(drawn, -most, most).astype(kind)


def setup_inputs(seed: int = 0) -> dict:
    streams_of = jax.random.split(jax.random.key(seed), 11)
    block_in = draw_block_in(jax.random.fold_in(streams_of[10], 71), 0)
    seq_lengths = draw_seq_lengths(jax.random.fold_in(streams_of[10], 71), 0)
    attn_gain = jnp.clip(1.0 + 0.15 * jax.random.normal(streams_of[2], (D,), jnp.float32), 0.25, 1.75).astype(jnp.bfloat16)
    qkv_weight = draw_qkv_weight(jax.random.fold_in(streams_of[10], 71), 0)
    out_weight = scatter_about(streams_of[4], (D, D), (D // 32) ** -0.5, 1.25, ((0, 4), (1, 8)))
    mlp_gain = jnp.clip(1.0 + 0.15 * jax.random.normal(streams_of[5], (D,), jnp.float32), 0.25, 1.75).astype(jnp.bfloat16)
    act_weight = scatter_about(streams_of[6], (D, FF), D ** -0.5, 0.21875, ((0, 8), (1, 4)))
    gate_weight = scatter_about(streams_of[7], (D, FF), D ** -0.5, 0.21875, ((0, 8), (1, 4)))
    down_weight = scatter_about(streams_of[8], (FF, D), (FF // 4) ** -0.5, 0.375, ((0, 4), (1, 8)))
    block_cot = draw_block_cot(jax.random.fold_in(streams_of[10], 71), 0)
    return {"block_in": block_in, "seq_lengths": seq_lengths, "attn_gain": attn_gain, "qkv_weight": qkv_weight, "out_weight": out_weight, "mlp_gain": mlp_gain, "act_weight": act_weight, "gate_weight": gate_weight, "down_weight": down_weight, "block_cot": block_cot}


EPSILON = 1e-05
THETA = 10000.0
NEGATIVE = -1e+30
ROOT_TWO = 1.4142135623730951
ROOT_TWO_PI = 2.5066282746310002

def seq_layout(lengths, count):
    finish = jnp.cumsum(lengths).astype(jnp.int32)
    places = jnp.arange(count, dtype=jnp.int32)
    passed = (places[:, None] >= finish[None, :]).astype(jnp.int32)
    segment = lax.optimization_barrier(jnp.sum(passed, axis=1)).astype(jnp.int32)
    opening = lax.optimization_barrier(jnp.sum(passed * lengths[None, :], axis=1)).astype(jnp.int32)
    return (segment, places - opening, segment < lengths.shape[0])

def norm_fwd(field):
    centre = field - lax.optimization_barrier(jnp.mean(field, axis=1, keepdims=True))
    inverse = lax.rsqrt(lax.optimization_barrier(jnp.mean(centre * centre, axis=1, keepdims=True)) + EPSILON)
    return (centre * inverse, inverse)

def norm_back(grad_norm, gain, unit, inverse):
    scaled = grad_norm * gain
    return inverse * (scaled - lax.optimization_barrier(jnp.mean(scaled, axis=1, keepdims=True)) - unit * lax.optimization_barrier(jnp.mean(scaled * unit, axis=1, keepdims=True)))

def gelu_parts(pre_value):
    normal_cdf = 0.5 * (1.0 + jax.scipy.special.erf(pre_value / ROOT_TWO))
    density = jnp.exp(-0.5 * pre_value * pre_value) / ROOT_TWO_PI
    return (pre_value * normal_cdf, normal_cdf + pre_value * density)

def rotary(position, width):
    half_width = width // 2
    freq = THETA ** (-2.0 * jnp.arange(half_width, dtype=jnp.float32) / width)
    angle = position.astype(jnp.float32)[:, None] * freq[None, :]
    return (jnp.concatenate([jnp.cos(angle), jnp.cos(angle)], axis=1), jnp.concatenate([jnp.sin(angle), jnp.sin(angle)], axis=1))

def rotate(field, cosine, sine):
    half_width = field.shape[-1] // 2
    turned = jnp.concatenate([-field[..., half_width:], field[..., :half_width]], axis=-1)
    return field * cosine[:, None, :] + turned * sine[:, None, :]

def rounded(value):
    return lax.optimization_barrier(value.astype(jnp.bfloat16)).astype(jnp.float32)

def window_mask(segment_q, segment_k, begin_row, span):
    places_q = begin_row + jnp.arange(span)
    places_k = begin_row - HALF + jnp.arange(span + 2 * HALF)
    near = jnp.abs(places_q[:, None] - places_k[None, :]) <= HALF
    return near & (segment_q[:, None] == segment_k[None, :])

def padded_inputs(keys, values, segment):
    edge = ((HALF, HALF), (0, 0), (0, 0))
    return (jnp.pad(keys, edge), jnp.pad(values, edge), jnp.pad(segment, (HALF, HALF), constant_values=-1))

def attend(query, keys, values, segment):
    count = query.shape[0]
    scale = HD ** (-0.5)
    keys_pad, values_pad, segment_pad = padded_inputs(keys, values, segment)
    results = []
    totals = []
    for begin_row in range(0, count, BLOCK):
        query_blk = query[begin_row:begin_row + BLOCK].astype(jnp.float32)
        keys_blk = keys_pad[begin_row:begin_row + BLOCK + 2 * HALF].astype(jnp.float32)
        values_blk = values_pad[begin_row:begin_row + BLOCK + 2 * HALF].astype(jnp.float32)
        allowed = window_mask(segment[begin_row:begin_row + BLOCK], segment_pad[begin_row:begin_row + BLOCK + 2 * HALF], begin_row, BLOCK)
        scores = jnp.where(allowed[None], jnp.einsum('qhe,khe->hqk', query_blk, keys_blk) * scale, NEGATIVE)
        peak = lax.optimization_barrier(jnp.max(scores, axis=2, keepdims=True))
        logsum = peak + jnp.log(lax.optimization_barrier(jnp.sum(jnp.exp(scores - peak), axis=2, keepdims=True)))
        probs = rounded(jnp.exp(scores - logsum))
        results.append(jnp.einsum('hqk,khe->qhe', probs, values_blk).astype(jnp.bfloat16))
        totals.append(logsum[:, :, 0])
    return (jnp.concatenate(results, axis=0), jnp.concatenate(totals, axis=1))

def attend_back(query, keys, values, attended, logsum, grad_att, segment):
    count = query.shape[0]
    scale = HD ** (-0.5)
    keys_pad, values_pad, segment_pad = padded_inputs(keys, values, segment)
    grad_keys = jnp.zeros(keys_pad.shape, jnp.float32)
    grad_values = jnp.zeros(values_pad.shape, jnp.float32)
    grad_query = []
    for begin_row in range(0, count, BLOCK):
        stop_row = begin_row + BLOCK
        wide_stop = begin_row + BLOCK + 2 * HALF
        query_blk = query[begin_row:stop_row].astype(jnp.float32)
        keys_blk = keys_pad[begin_row:wide_stop].astype(jnp.float32)
        values_blk = values_pad[begin_row:wide_stop].astype(jnp.float32)
        allowed = window_mask(segment[begin_row:stop_row], segment_pad[begin_row:wide_stop], begin_row, BLOCK)
        scores = jnp.where(allowed[None], jnp.einsum('qhe,khe->hqk', query_blk, keys_blk) * scale, NEGATIVE)
        probs = jnp.exp(scores - logsum[:, begin_row:stop_row][:, :, None])
        grad_blk = grad_att[begin_row:stop_row].astype(jnp.float32)
        att_blk = attended[begin_row:stop_row].astype(jnp.float32)
        grad_values = grad_values.at[begin_row:wide_stop].add(jnp.einsum('hqk,qhe->khe', rounded(probs), grad_blk))
        grad_probs = jnp.einsum('qhe,khe->hqk', grad_blk, values_blk)
        delta = lax.optimization_barrier(jnp.sum(grad_blk * att_blk, axis=2)).T
        grad_scores = rounded(probs * (grad_probs - delta[:, :, None]) * scale)
        grad_query.append(jnp.einsum('hqk,khe->qhe', grad_scores, keys_blk))
        grad_keys = grad_keys.at[begin_row:wide_stop].add(jnp.einsum('hqk,qhe->khe', grad_scores, query_blk))
    return (jnp.concatenate(grad_query, axis=0), grad_keys[HALF:HALF + count], grad_values[HALF:HALF + count])

def inner(left, right):
    return lax.dot_general(left, right, (((0,), (0,)), ((), ())), preferred_element_type=jnp.float32)

def outer(left, right):
    return lax.dot_general(left, right, (((1,), (1,)), ((), ())), preferred_element_type=jnp.float32)

def split_dot(left, right):
    width = left.shape[1] // N_TENSOR
    total = jnp.zeros((left.shape[0], right.shape[1]), jnp.float32)
    for index in range(N_TENSOR):
        lower = index * width
        term = jnp.dot(left[:, lower:lower + width], right[lower:lower + width], preferred_element_type=jnp.float32)
        total = total + rounded(term)
    return total

def split_outer(pairs):
    width = pairs[0][0].shape[1] // N_TENSOR
    total = jnp.zeros((pairs[0][0].shape[0], pairs[0][1].shape[0]), jnp.float32)
    for index in range(N_TENSOR):
        lower = index * width
        term = jnp.zeros_like(total)
        for left, right in pairs:
            term = term + outer(left[:, lower:lower + width], right[:, lower:lower + width])
        total = total + rounded(term)
    return total

def reference(block_in, seq_lengths, attn_gain, qkv_weight, out_weight, mlp_gain, act_weight, gate_weight, down_weight, block_cot):
    gain_one = attn_gain.astype(jnp.float32)
    gain_two = mlp_gain.astype(jnp.float32)

    def group_step(totals, item):
        rows_in, cot_in, lengths = item
        segment, position, valid = seq_layout(lengths, TOK_DEV)
        keep = valid.astype(jnp.float32)[:, None]
        field = rows_in.astype(jnp.float32)
        unit1, inverse1 = norm_fwd(field)
        normed1 = (unit1 * gain_one).astype(jnp.bfloat16)
        mixed = jnp.dot(normed1, qkv_weight, preferred_element_type=jnp.float32).reshape(TOK_DEV, HEADS, 3, HD)
        cosine, sine = rotary(position, HD)
        query = rotate(mixed[:, :, 0], cosine, sine).astype(jnp.bfloat16)
        keys = rotate(mixed[:, :, 1], cosine, sine).astype(jnp.bfloat16)
        values = mixed[:, :, 2].astype(jnp.bfloat16)
        attended, logsum = attend(query, keys, values, segment)
        merged = attended.reshape(TOK_DEV, D)
        hidden_res = field + split_dot(merged, out_weight)
        unit2, inverse2 = norm_fwd(hidden_res)
        normed2 = (unit2 * gain_two).astype(jnp.bfloat16)
        pre_act = jnp.dot(normed2, act_weight, preferred_element_type=jnp.float32)
        pre_gate = jnp.dot(normed2, gate_weight, preferred_element_type=jnp.float32)
        gelu_val, gelu_slope = gelu_parts(pre_act)
        product = (gelu_val * pre_gate).astype(jnp.bfloat16)
        block_rows = ((hidden_res + split_dot(product, down_weight)) * keep).astype(jnp.bfloat16)
        upstream = (cot_in.astype(jnp.float32) * keep).astype(jnp.bfloat16)
        down_part = inner(product, upstream)
        grad_prod = outer(upstream, down_weight)
        grad_act = (grad_prod * pre_gate * gelu_slope).astype(jnp.bfloat16)
        grad_gate = (grad_prod * gelu_val).astype(jnp.bfloat16)
        act_part = inner(normed2, grad_act)
        gate_part = inner(normed2, grad_gate)
        grad_norm2 = split_outer(((grad_act, act_weight), (grad_gate, gate_weight)))
        gain2_part = lax.optimization_barrier(jnp.sum(grad_norm2 * unit2, axis=0))
        grad_res = upstream.astype(jnp.float32) + norm_back(grad_norm2, gain_two, unit2, inverse2)
        grad_res_b = grad_res.astype(jnp.bfloat16)
        out_part = inner(merged, grad_res_b)
        grad_att = outer(grad_res_b, out_weight).astype(jnp.bfloat16).reshape(TOK_DEV, HEADS, HD)
        grad_query, grad_keys, grad_values = attend_back(query, keys, values, attended, logsum, grad_att, segment)
        grad_mixed = jnp.stack([rotate(grad_query, cosine, -sine), rotate(grad_keys, cosine, -sine), grad_values], axis=2)
        grad_mixed = grad_mixed.astype(jnp.bfloat16).reshape(TOK_DEV, 3 * D)
        qkv_part = inner(normed1, grad_mixed)
        grad_norm1 = split_outer(((grad_mixed, qkv_weight),))
        gain1_part = lax.optimization_barrier(jnp.sum(grad_norm1 * unit1, axis=0))
        grad_rows = (grad_res + norm_back(grad_norm1, gain_one, unit1, inverse1)) * keep
        new_totals = (totals[0] + gain1_part, totals[1] + qkv_part, totals[2] + out_part, totals[3] + gain2_part, totals[4] + act_part, totals[5] + gate_part, totals[6] + down_part)
        return (new_totals, (block_rows, grad_rows))
    start_totals = (jnp.zeros((D,), jnp.float32), jnp.zeros((D, 3 * D), jnp.float32), jnp.zeros((D, D), jnp.float32), jnp.zeros((D,), jnp.float32), jnp.zeros((D, FF), jnp.float32), jnp.zeros((D, FF), jnp.float32), jnp.zeros((FF, D), jnp.float32))
    items = (block_in.reshape(N_DP, TOK_DEV, D), block_cot.reshape(N_DP, TOK_DEV, D), seq_lengths)
    totals, stacked = lax.scan(group_step, start_totals, items)
    block_out = stacked[0].reshape(TOKENS, D)
    input_grad = stacked[1].reshape(TOKENS, D)
    return (block_out, input_grad, totals[0], totals[1], totals[2], totals[3], totals[4], totals[5], totals[6])
```

```python
import functools

import jax
import jax.numpy as jnp
from jax import lax
from jax.experimental import pallas as pl
from jax.experimental.pallas import tpu as pltpu
from jax.sharding import PartitionSpec as P

HD = 64
HALF = 64
BLOCK = 512


EPSILON = 1e-05
THETA = 10000.0
NEGATIVE = -1e30
ROOT_TWO = 1.4142135623730951
ROOT_TWO_PI = 2.5066282746310002


def seq_layout(lengths, count):
    finish = jnp.cumsum(lengths)
    places = jnp.arange(count, dtype=jnp.int32)
    passed = (places[:, None] >= finish[None, :]).astype(jnp.int32)
    segment = jnp.sum(passed, axis=1)
    opening = jnp.sum(passed * lengths[None, :], axis=1)
    return (segment, places - opening, segment < lengths.shape[0])


def norm_fwd(field):
    centre = field - jnp.mean(field, axis=1, keepdims=True)
    inverse = lax.rsqrt(jnp.mean(centre * centre, axis=1, keepdims=True) + EPSILON)
    return (centre * inverse, inverse)


def norm_back(grad_norm, gain, unit, inverse):
    scaled = grad_norm * gain
    return inverse * (
        scaled
        - jnp.mean(scaled, axis=1, keepdims=True)
        - unit * jnp.mean(scaled * unit, axis=1, keepdims=True)
    )


def gelu_parts(pre_value):
    normal_cdf = 0.5 * (1.0 + jax.scipy.special.erf(pre_value / ROOT_TWO))
    density = jnp.exp(-0.5 * pre_value * pre_value) / ROOT_TWO_PI
    return (pre_value * normal_cdf, normal_cdf + pre_value * density)


def rotary(position, width):
    half_width = width // 2
    freq = THETA ** (-2.0 * jnp.arange(half_width, dtype=jnp.float32) / width)
    angle = position.astype(jnp.float32)[:, None] * freq[None, :]
    return (
        jnp.concatenate([jnp.cos(angle), jnp.cos(angle)], axis=1),
        jnp.concatenate([jnp.sin(angle), jnp.sin(angle)], axis=1),
    )


def rotate(field, cosine, sine):
    half_width = field.shape[-1] // 2
    turned = jnp.concatenate([-field[..., half_width:], field[..., :half_width]], axis=-1)
    return field * cosine[:, None, :] + turned * sine[:, None, :]


def window_mask(segment_q, segment_k, begin_row, span):
    places_q = begin_row + jnp.arange(span)
    places_k = begin_row - HALF + jnp.arange(span + 2 * HALF)
    near = jnp.abs(places_q[:, None] - places_k[None, :]) <= HALF
    return near & (segment_q[:, None] == segment_k[None, :])


def padded_inputs(keys, values, segment):
    edge = ((HALF, HALF), (0, 0), (0, 0))
    return (
        jnp.pad(keys, edge),
        jnp.pad(values, edge),
        jnp.pad(segment, (HALF, HALF), constant_values=-1),
    )


def attend(query, keys, values, segment):
    count = query.shape[0]
    scale = HD ** (-0.5)
    keys_pad, values_pad, segment_pad = padded_inputs(keys, values, segment)
    results = []
    totals = []
    for begin_row in range(0, count, BLOCK):
        wide_stop = begin_row + BLOCK + 2 * HALF
        allowed = window_mask(
            segment[begin_row : begin_row + BLOCK],
            segment_pad[begin_row:wide_stop],
            begin_row,
            BLOCK,
        )
        scores = (
            jnp.einsum(
                "qhe,khe->hqk",
                query[begin_row : begin_row + BLOCK],
                keys_pad[begin_row:wide_stop],
                preferred_element_type=jnp.float32,
            )
            * scale
        )
        scores = jnp.where(allowed[None], scores, NEGATIVE)
        peak = jnp.max(scores, axis=2, keepdims=True)
        logsum = peak + jnp.log(jnp.sum(jnp.exp(scores - peak), axis=2, keepdims=True))
        probs = jnp.exp(scores - logsum).astype(jnp.bfloat16)
        results.append(
            jnp.einsum(
                "hqk,khe->qhe",
                probs,
                values_pad[begin_row:wide_stop],
                preferred_element_type=jnp.float32,
            ).astype(jnp.bfloat16)
        )
        totals.append(logsum[:, :, 0])
    return (jnp.concatenate(results, axis=0), jnp.concatenate(totals, axis=1))


def attend_back(query, keys, values, attended, logsum, grad_att, segment):
    count = query.shape[0]
    scale = HD ** (-0.5)
    keys_pad, values_pad, segment_pad = padded_inputs(keys, values, segment)
    grad_keys = jnp.zeros(keys_pad.shape, jnp.float32)
    grad_values = jnp.zeros(values_pad.shape, jnp.float32)
    grad_query = []
    for begin_row in range(0, count, BLOCK):
        stop_row = begin_row + BLOCK
        wide_stop = begin_row + BLOCK + 2 * HALF
        query_blk = query[begin_row:stop_row]
        keys_blk = keys_pad[begin_row:wide_stop]
        allowed = window_mask(
            segment[begin_row:stop_row], segment_pad[begin_row:wide_stop], begin_row, BLOCK
        )
        scores = (
            jnp.einsum("qhe,khe->hqk", query_blk, keys_blk, preferred_element_type=jnp.float32)
            * scale
        )
        scores = jnp.where(allowed[None], scores, NEGATIVE)
        probs = jnp.exp(scores - logsum[:, begin_row:stop_row][:, :, None])
        grad_blk = grad_att[begin_row:stop_row]
        grad_values = grad_values.at[begin_row:wide_stop].add(
            jnp.einsum(
                "hqk,qhe->khe",
                probs.astype(jnp.bfloat16),
                grad_blk,
                preferred_element_type=jnp.float32,
            )
        )
        grad_probs = jnp.einsum(
            "qhe,khe->hqk",
            grad_blk,
            values_pad[begin_row:wide_stop],
            preferred_element_type=jnp.float32,
        )
        delta = jnp.sum(
            grad_blk.astype(jnp.float32) * attended[begin_row:stop_row].astype(jnp.float32), axis=2
        ).T
        grad_scores = (probs * (grad_probs - delta[:, :, None]) * scale).astype(jnp.bfloat16)
        grad_query.append(
            jnp.einsum("hqk,khe->qhe", grad_scores, keys_blk, preferred_element_type=jnp.float32)
        )
        grad_keys = grad_keys.at[begin_row:wide_stop].add(
            jnp.einsum("hqk,qhe->khe", grad_scores, query_blk, preferred_element_type=jnp.float32)
        )
    return (
        jnp.concatenate(grad_query, axis=0),
        grad_keys[HALF : HALF + count],
        grad_values[HALF : HALF + count],
    )


def inner(left, right):
    return lax.dot_general(
        left, right, (((0,), (0,)), ((), ())), preferred_element_type=jnp.float32
    )


def outer(left, right):
    return lax.dot_general(
        left, right, (((1,), (1,)), ((), ())), preferred_element_type=jnp.float32
    )


def on_device(
    block_in,
    seq_lengths,
    attn_gain,
    qkv_weight,
    out_weight,
    mlp_gain,
    act_weight,
    gate_weight,
    down_weight,
    block_cot,
):
    local_rows = block_in.shape[0]
    group_rows = local_rows * lax.axis_size("tensor")
    segment, position, valid = seq_layout(seq_lengths[0], group_rows)
    my_offset = lax.axis_index("tensor") * local_rows
    keep_local = lax.dynamic_slice_in_dim(valid, my_offset, local_rows, 0).astype(jnp.float32)[
        :, None
    ]
    gathered = (
        lax.all_gather(qkv_weight, "dp", axis=0, tiled=True),
        lax.all_gather(out_weight, "dp", axis=1, tiled=True),
        lax.all_gather(attn_gain, "dp", axis=0, tiled=True),
        lax.all_gather(mlp_gain, "dp", axis=0, tiled=True),
        lax.all_gather(act_weight, "dp", axis=0, tiled=True),
        lax.all_gather(gate_weight, "dp", axis=0, tiled=True),
        lax.all_gather(down_weight, "dp", axis=1, tiled=True),
    )
    full_qkv, full_out, gain_whole1, gain_whole2, full_act, full_gate, full_down = gathered
    gain_one = gain_whole1.astype(jnp.float32)
    gain_two = gain_whole2.astype(jnp.float32)
    heads_here = full_qkv.shape[1] // (3 * HD)
    field = block_in.astype(jnp.float32)
    unit1, inverse1 = norm_fwd(field)
    normed1 = lax.all_gather((unit1 * gain_one).astype(jnp.bfloat16), "tensor", axis=0, tiled=True)
    mixed = jnp.dot(normed1, full_qkv, preferred_element_type=jnp.float32).reshape(
        group_rows, heads_here, 3, HD
    )
    cosine, sine = rotary(position, HD)
    query = rotate(mixed[:, :, 0], cosine, sine).astype(jnp.bfloat16)
    keys = rotate(mixed[:, :, 1], cosine, sine).astype(jnp.bfloat16)
    values = mixed[:, :, 2].astype(jnp.bfloat16)
    attended, logsum = attend(query, keys, values, segment)
    merged = attended.reshape(group_rows, heads_here * HD)
    hidden_res = field + lax.psum_scatter(
        jnp.dot(merged, full_out, preferred_element_type=jnp.float32).astype(jnp.bfloat16),
        "tensor",
        scatter_dimension=0,
        tiled=True,
    ).astype(jnp.float32)
    unit2, inverse2 = norm_fwd(hidden_res)
    normed2 = lax.all_gather((unit2 * gain_two).astype(jnp.bfloat16), "tensor", axis=0, tiled=True)
    pre_act = jnp.dot(normed2, full_act, preferred_element_type=jnp.float32)
    pre_gate = jnp.dot(normed2, full_gate, preferred_element_type=jnp.float32)
    gelu_val, gelu_slope = gelu_parts(pre_act)
    product = (gelu_val * pre_gate).astype(jnp.bfloat16)
    block_out = (
        (
            hidden_res
            + lax.psum_scatter(
                jnp.dot(product, full_down, preferred_element_type=jnp.float32).astype(
                    jnp.bfloat16
                ),
                "tensor",
                scatter_dimension=0,
                tiled=True,
            ).astype(jnp.float32)
        )
        * keep_local
    ).astype(jnp.bfloat16)
    again = (
        lax.all_gather(qkv_weight, "dp", axis=0, tiled=True),
        lax.all_gather(out_weight, "dp", axis=1, tiled=True),
        lax.all_gather(act_weight, "dp", axis=0, tiled=True),
        lax.all_gather(gate_weight, "dp", axis=0, tiled=True),
        lax.all_gather(down_weight, "dp", axis=1, tiled=True),
    )
    back_qkv, back_out, back_act, back_gate, back_down = again
    upstream_local = (block_cot.astype(jnp.float32) * keep_local).astype(jnp.bfloat16)
    upstream = lax.all_gather(upstream_local, "tensor", axis=0, tiled=True)
    down_part = inner(product, upstream)
    grad_prod = outer(upstream, back_down)
    grad_act = (grad_prod * pre_gate * gelu_slope).astype(jnp.bfloat16)
    grad_gate = (grad_prod * gelu_val).astype(jnp.bfloat16)
    act_part = inner(normed2, grad_act)
    gate_part = inner(normed2, grad_gate)
    grad_norm2 = lax.psum_scatter(
        (outer(grad_act, back_act) + outer(grad_gate, back_gate)).astype(jnp.bfloat16),
        "tensor",
        scatter_dimension=0,
        tiled=True,
    ).astype(jnp.float32)
    gain2_part = jnp.sum(grad_norm2 * unit2, axis=0)
    grad_res = upstream_local.astype(jnp.float32) + norm_back(grad_norm2, gain_two, unit2, inverse2)
    grad_rows = lax.all_gather(grad_res.astype(jnp.bfloat16), "tensor", axis=0, tiled=True)
    out_part = inner(merged, grad_rows)
    grad_att = outer(grad_rows, back_out).astype(jnp.bfloat16).reshape(group_rows, heads_here, HD)
    grad_query, grad_keys, grad_values = attend_back(
        query, keys, values, attended, logsum, grad_att, segment
    )
    grad_mixed = jnp.stack(
        [rotate(grad_query, cosine, -sine), rotate(grad_keys, cosine, -sine), grad_values], axis=2
    )
    grad_mixed = grad_mixed.astype(jnp.bfloat16).reshape(group_rows, heads_here * 3 * HD)
    qkv_part = inner(normed1, grad_mixed)
    grad_norm1 = lax.psum_scatter(
        outer(grad_mixed, back_qkv).astype(jnp.bfloat16), "tensor", scatter_dimension=0, tiled=True
    ).astype(jnp.float32)
    gain1_part = jnp.sum(grad_norm1 * unit1, axis=0)
    input_grad = (grad_res + norm_back(grad_norm1, gain_one, unit1, inverse1)) * keep_local
    qkv_grad, out_grad, gain1_share, act_grad, gate_grad, down_grad, gain2_share = (
        lax.psum_scatter(qkv_part, "dp", scatter_dimension=0, tiled=True),
        lax.psum_scatter(out_part, "dp", scatter_dimension=1, tiled=True),
        lax.psum_scatter(gain1_part, "dp", scatter_dimension=0, tiled=True),
        lax.psum_scatter(act_part, "dp", scatter_dimension=0, tiled=True),
        lax.psum_scatter(gate_part, "dp", scatter_dimension=0, tiled=True),
        lax.psum_scatter(down_part, "dp", scatter_dimension=1, tiled=True),
        lax.psum_scatter(gain2_part, "dp", scatter_dimension=0, tiled=True),
    )
    attn_gain_grad, mlp_gain_grad = lax.psum((gain1_share, gain2_share), "tensor")
    return (
        block_out,
        input_grad,
        attn_gain_grad,
        qkv_grad,
        out_grad,
        mlp_gain_grad,
        act_grad,
        gate_grad,
        down_grad,
    )


QROWS = 128
NN = (((1,), (0,)), ((), ()))
NT = (((1,), (1,)), ((), ()))
TN = (((0,), (0,)), ((), ()))


def mm(left, right, dims=NN):
    return lax.dot_general(left, right, dims, preferred_element_type=jnp.float32)


def swap(value, dp_mask=0, tensor_mask=0):
    dp_size, tensor_size = lax.axis_size("dp"), lax.axis_size("tensor")
    if not tensor_mask:
        return lax.ppermute(value, "dp", [(i, i ^ dp_mask) for i in range(dp_size)])
    if not dp_mask:
        return lax.ppermute(value, "tensor", [(i, i ^ tensor_mask) for i in range(tensor_size)])
    pairs = [
        (d * tensor_size + t, (d ^ dp_mask) * tensor_size + (t ^ tensor_mask))
        for d in range(dp_size)
        for t in range(tensor_size)
    ]
    return lax.ppermute(value, ("dp", "tensor"), pairs)


def gather_all(pack):
    deep = lax.axis_size("dp") // 2
    mine = jnp.stack([pack] + [swap(pack, 2 * j) for j in range(1, deep)])
    same_core = [mine, swap(mine, 0, 2), swap(mine, 1, 0), swap(mine, 1, 2)]
    return same_core + [swap(piece, 0, 1) for piece in same_core]


PIECES = ((0, 0), (0, 2), (1, 0), (1, 2), (0, 1), (0, 3), (1, 1), (1, 3))


def reduce_all(keep, send):
    deep = lax.axis_size("dp") // 2
    got = swap(send, 0, 1)
    rows = keep.shape[0] // 4
    pairs = [
        (
            keep[k * rows : (k + 1) * rows].astype(jnp.float32)
            + got[k * rows : (k + 1) * rows].astype(jnp.float32)
        ).astype(jnp.bfloat16)
        for k in range(4)
    ]
    from_y, from_x, from_xy = swap(pairs[1], 1, 0), swap(pairs[2], 0, 2), swap(pairs[3], 1, 2)
    layer = (pairs[0].astype(jnp.float32) + from_x.astype(jnp.float32)) + (
        from_y.astype(jnp.float32) + from_xy.astype(jnp.float32)
    )
    layer = layer.astype(jnp.bfloat16)
    rows = rows // deep
    total = layer[:rows].astype(jnp.float32)
    for j in range(1, deep):
        total = total + swap(layer[j * rows : (j + 1) * rows], 2 * j).astype(jnp.float32)
    return total


def unit_of(field):
    centre = field - jnp.mean(field, axis=1, keepdims=True)
    inverse = lax.rsqrt(jnp.mean(centre * centre, axis=1, keepdims=True) + EPSILON)
    return centre * inverse, inverse


def unpack_weights(place_ref, pieces, full_ref, rows):
    for (y_bit, tensor_mask), piece in zip(PIECES, pieces):
        for j in range(piece.shape[0]):
            begin = pl.multiple_of((place_ref[0] ^ (2 * j + y_bit)) * rows, rows)
            full_ref[tensor_mask, pl.ds(begin, rows), :] = piece[j, :rows, :]


def half_turn(tile):
    lane = lax.broadcasted_iota(jnp.int32, tile.shape, 1)
    return jnp.where((lane & (HD // 2)) == 0, pltpu.roll(tile, 128 - HD // 2, 1), pltpu.roll(tile, HD // 2, 1))


def turn_tiles(field, cos_ref, sin_ref, sign):
    width = field.shape[1]
    period = cos_ref.shape[1]
    parts = []
    for begin in range(0, width, 128):
        tile = field[:, begin : begin + 128]
        if tile.shape[1] == 128:
            at = begin % period
            side = half_turn(tile) * sin_ref[:, at : at + 128]
            base = tile * cos_ref[:, at : at + 128]
            tile = base + side if sign > 0 else base - side
        parts.append(tile)
    return parts


def attention_kernel(rows, place_ref, edge_l, block, edge_r, cos_ref, sin_ref, *refs):
    pieces = refs[:8]
    full_ref, mixed_ref, probs_ref, att_ref, res_ref, gain_ref, gains_s = refs[8:]
    own = block.shape[0]
    wide = own + 2 * HALF
    unpack_weights(place_ref, pieces, full_ref, rows)
    for y_bit in range(2):
        piece = pieces[2 * y_bit]
        for j in range(piece.shape[0]):
            gains_s[place_ref[0] ^ (2 * j + y_bit)] = piece[j, rows : rows + 8, :rows].astype(jnp.float32)
    for i in range(gains_s.shape[0]):
        gain_ref[:, i * rows : (i + 1) * rows] = gains_s[i]
    field = jnp.concatenate([edge_l[...], block[...], edge_r[...]], axis=0).astype(jnp.float32)
    unit, _ = unit_of(field)
    normed = (unit * gain_ref[0:1, :]).astype(jnp.bfloat16)
    first = place_ref[1] * own - HALF
    total = place_ref[3]
    allowed = []
    for b in range(own // QROWS):
        span = QROWS + 2 * HALF
        i = first + HALF + b * QROWS + lax.broadcasted_iota(jnp.int32, (QROWS, span), 0)
        j = first + b * QROWS + lax.broadcasted_iota(jnp.int32, (QROWS, span), 1)
        same = (i < place_ref[2]) == (j < place_ref[2])
        allowed.append((jnp.abs(i - j) <= HALF) & same & (j >= 0) & (j < total))
    outer_cols = full_ref.shape[2]
    qkv_cols = mixed_ref.shape[2]
    heads = qkv_cols // (3 * HD)
    result = field[HALF : HALF + own]
    for t in range(4):
        mixed = mm(normed, full_ref[t, :, :qkv_cols])
        begin = 0
        for part in turn_tiles(mixed, cos_ref, sin_ref, 1):
            mixed_ref[t, :, begin : begin + part.shape[1]] = part.astype(jnp.bfloat16)
            begin += part.shape[1]
        for h in range(heads):
            at = h * 3 * HD
            for b in range(own // QROWS):
                low = b * QROWS
                span = slice(low, low + QROWS + 2 * HALF)
                query = mixed_ref[t, HALF + low : HALF + low + QROWS, at : at + HD]
                keys = mixed_ref[t, span, at + HD : at + 2 * HD]
                values = mixed_ref[t, span, at + 2 * HD : at + 3 * HD]
                scores = jnp.where(allowed[b], mm(query, keys, NT) * HD ** (-0.5), NEGATIVE)
                peak = jnp.max(scores, axis=1, keepdims=True)
                grown = jnp.exp(scores - peak)
                probs = (grown * (1.0 / jnp.sum(grown, axis=1, keepdims=True))).astype(jnp.bfloat16)
                probs_ref[t * heads + h, b] = probs
                att_ref[low : low + QROWS, (t * heads + h) * HD : (t * heads + h + 1) * HD] = mm(
                    probs, values
                ).astype(jnp.bfloat16)
        result = result + mm(
            att_ref[:, t * heads * HD : (t + 1) * heads * HD], full_ref[t, :, qkv_cols:outer_cols], NT
        )
    res_ref[...] = result


def relative_rows(place_ref, flipped, out_ref, rows):
    deep = out_ref.shape[0] // rows // 2
    for y_bit in range(2):
        for j in range(deep):
            begin = pl.multiple_of((place_ref[0] ^ (2 * j + y_bit)) * rows, rows)
            to = (y_bit * deep + j) * rows
            out_ref[to : to + rows, :] = flipped[pl.ds(begin, rows), :]


def feed_kernel(rows, place_ref, res_ref, cot_ref, gain_ref, att_ref, attw_ref, *refs):
    pieces = refs[:8]
    out_ref, grad_ref, gatt_ref, gain2_ref, keep_ref, send_ref, full_ref, flip_n, flip_u, flip_s, rel_n, rel_u = refs[8:]
    own, width = res_ref.shape
    unpack_weights(place_ref, pieces, full_ref, rows)
    row = place_ref[1] * own + lax.broadcasted_iota(jnp.int32, (own, 1), 0)
    keep = (row < place_ref[2]).astype(jnp.float32)
    field = res_ref[...]
    unit, inverse = unit_of(field)
    gain = gain_ref[1:2, :]
    normed_f = unit * gain
    normed = normed_f.astype(jnp.bfloat16)
    upstream_f = cot_ref[...].astype(jnp.float32) * keep
    upstream = upstream_f.astype(jnp.bfloat16)
    flip_n[...] = normed_f.T.astype(jnp.bfloat16)
    relative_rows(place_ref, flip_n, rel_n, rows)
    flip_u[...] = upstream_f.T.astype(jnp.bfloat16)
    relative_rows(place_ref, flip_u, rel_u, rows)
    units = full_ref.shape[2] // 3
    result = field
    grad_norm = jnp.zeros((own, width), jnp.float32)
    for t in range(4):
        dest = (keep_ref, send_ref)[t & 1]
        to = slice((t >> 1) * width, (t >> 1) * width + width)
        pre = mm(normed, full_ref[t, :, : 2 * units])
        pre_act, pre_gate = pre[:, :units], pre[:, units:]
        cdf = 0.5 * (1.0 + lax.erf(pre_act / ROOT_TWO))
        density = jnp.exp(-0.5 * pre_act * pre_act) / ROOT_TWO_PI
        gelu_val = pre_act * cdf
        product = (gelu_val * pre_gate).astype(jnp.bfloat16)
        down = full_ref[t, :, 2 * units :]
        result = result + mm(product, down, NT)
        grad_prod = mm(upstream, down)
        grad_act = (grad_prod * pre_gate * (cdf + pre_act * density)).astype(jnp.bfloat16)
        grad_gate = (grad_prod * gelu_val).astype(jnp.bfloat16)
        both = jnp.concatenate([grad_act, grad_gate], axis=1)
        grad_norm = grad_norm + mm(both, full_ref[t, :, : 2 * units], NT)
        dest[to, : 2 * units] = mm(rel_n[...], both).astype(jnp.bfloat16)
        dest[to, 2 * units : 3 * units] = mm(rel_u[...], product).astype(jnp.bfloat16)
    out_ref[...] = (result * keep).astype(jnp.bfloat16)
    gain2_ref[...] = jnp.sum(grad_norm * unit, axis=0, keepdims=True)
    grad_res = upstream_f + norm_back(grad_norm, gain, unit, inverse)
    grad_ref[...] = grad_res
    grad_rows = grad_res.astype(jnp.bfloat16)
    flip_s[...] = grad_res.T.astype(jnp.bfloat16)
    relative_rows(place_ref, flip_s, rel_u, rows)
    head_cols = att_ref.shape[1] // 4
    skip = attw_ref.shape[2] - head_cols
    for t in range(4):
        dest = (keep_ref, send_ref)[t & 1]
        to = slice((t >> 1) * width, (t >> 1) * width + width)
        cols = slice(t * head_cols, (t + 1) * head_cols)
        dest[to, 3 * units :] = mm(rel_u[...], att_ref[:, cols]).astype(jnp.bfloat16)
        gatt_ref[:, cols] = mm(grad_rows, attw_ref[t, :, skip:]).astype(jnp.bfloat16)


def attention_back_kernel(mixed_ref, probs_ref, att_ref, gatt_ref, cos_ref, sin_ref, own_ref, edge_l, edge_r, grads):
    own = att_ref.shape[0]
    qkv_cols = mixed_ref.shape[2]
    heads = qkv_cols // (3 * HD)
    span = QROWS + 2 * HALF
    for t in range(4):
        grads[...] = jnp.zeros(grads.shape, jnp.float32)
        for h in range(heads):
            at = h * 3 * HD
            cols = slice((t * heads + h) * HD, (t * heads + h + 1) * HD)
            for b in range(own // QROWS):
                low = b * QROWS
                wide = slice(low, low + span)
                query = mixed_ref[t, HALF + low : HALF + low + QROWS, at : at + HD]
                keys = mixed_ref[t, wide, at + HD : at + 2 * HD]
                values = mixed_ref[t, wide, at + 2 * HD : at + 3 * HD]
                probs = probs_ref[t * heads + h, b]
                grad_att = gatt_ref[low : low + QROWS, cols]
                delta = jnp.sum(
                    grad_att.astype(jnp.float32) * att_ref[low : low + QROWS, cols].astype(jnp.float32),
                    axis=1,
                    keepdims=True,
                )
                grad_probs = mm(grad_att, values, NT)
                grad_scores = (probs.astype(jnp.float32) * (grad_probs - delta) * HD ** (-0.5)).astype(jnp.bfloat16)
                grads[HALF + low : HALF + low + QROWS, at : at + HD] = mm(grad_scores, keys)
                grads[wide, at + HD : at + 2 * HD] += mm(grad_scores, query, TN)
                grads[wide, at + 2 * HD : at + 3 * HD] += mm(probs, grad_att, TN)
        begin = 0
        for part in turn_tiles(grads[...], cos_ref, sin_ref, -1):
            own_ref[:, t * qkv_cols + begin : t * qkv_cols + begin + part.shape[1]] = part[HALF : HALF + own]
            edge_l[t, :, begin : begin + part.shape[1]] = part[:HALF].astype(jnp.bfloat16)
            edge_r[t, :, begin : begin + part.shape[1]] = part[HALF + own :].astype(jnp.bfloat16)
            begin += part.shape[1]


def finish_kernel(
    rows, place_ref, block, gain_ref, gain2_ref, res_ref, own_ref, edge_l, edge_r, full_ref, in_ref, keep_ref, send_ref, flip_s, rel_n, gains_s
):
    own, width = block.shape
    deep = keep_ref.shape[0] // 4 // (rows + 8)
    unit, inverse = unit_of(block[...].astype(jnp.float32))
    gain = gain_ref[0:1, :]
    flip_s[...] = (unit * gain).T.astype(jnp.bfloat16)
    relative_rows(place_ref, flip_s, rel_n, rows)
    qkv_cols = own_ref.shape[1] // 4
    grad_norm = jnp.zeros((own, width), jnp.float32)
    me = place_ref[1]
    to_left, to_right = me ^ ((me - 1) & 3), me ^ ((me + 1) & 3)
    for t in range(4):
        dest = (keep_ref, send_ref)[t & 1]
        cols = slice(t * qkv_cols, (t + 1) * qkv_cols)
        mixed = own_ref[:, cols]
        mixed = jnp.concatenate(
            [
                mixed[:HALF] + edge_l[t ^ to_left].astype(jnp.float32),
                mixed[HALF : own - HALF],
                mixed[own - HALF :] + edge_r[t ^ to_right].astype(jnp.float32),
            ],
            axis=0,
        ).astype(jnp.bfloat16)
        part = mm(rel_n[...], mixed).astype(jnp.bfloat16)
        for k in range(2 * deep):
            to = ((t >> 1) * 2 * deep + k) * (rows + 8)
            dest[to : to + rows, :] = part[k * rows : (k + 1) * rows]
        grad_norm = grad_norm + mm(mixed, full_ref[t, :, :qkv_cols], NT)
    gain1 = jnp.sum(grad_norm * unit, axis=0, keepdims=True)
    both = jnp.concatenate([gain1, gain2_ref[...], jnp.zeros((6, width), jnp.float32)], axis=0)
    for i in range(2 * deep):
        gains_s[i, :, :rows] = both[:, i * rows : (i + 1) * rows]
    for y_bit in range(2):
        for j in range(deep):
            share = gains_s[place_ref[0] ^ (2 * j + y_bit)].astype(jnp.bfloat16)
            for t in range(4):
                dest = (keep_ref, send_ref)[t & 1]
                to = ((t >> 1) * 2 * deep + y_bit * deep + j) * (rows + 8) + rows
                dest[to : to + 8, :] = jnp.concatenate(
                    [share, jnp.zeros((8, dest.shape[1] - share.shape[1]), jnp.bfloat16)], axis=1
                )
    row = place_ref[1] * own + lax.broadcasted_iota(jnp.int32, (own, 1), 0)
    valid = (row < place_ref[2]).astype(jnp.float32)
    in_ref[...] = (res_ref[...] + norm_back(grad_norm, gain, unit, inverse)) * valid


def call(kernel, name, n_in, outs, scratch, flops=0, moved=0):
    specs = [pl.BlockSpec(memory_space=pltpu.VMEM)] * n_in
    return pl.pallas_call(
        kernel,
        name=name,
        out_shape=outs,
        in_specs=[pl.BlockSpec(memory_space=pltpu.SMEM)] + specs if name != "attention_back" else specs,
        out_specs=[pl.BlockSpec(memory_space=pltpu.VMEM)] * len(outs),
        scratch_shapes=scratch,
        cost_estimate=pl.CostEstimate(flops=flops, bytes_accessed=moved, transcendentals=0),
        compiler_params=pltpu.CompilerParams(vmem_limit_bytes=56 * 1024 * 1024),
    )


def on_device_tokens(
    block_in,
    seq_lengths,
    attn_gain,
    qkv_weight,
    out_weight,
    mlp_gain,
    act_weight,
    gate_weight,
    down_weight,
    block_cot,
):
    own, width = block_in.shape
    tensor_size, dp_size = lax.axis_size("tensor"), lax.axis_size("dp")
    rows, qkv_cols = qkv_weight.shape
    head_cols, units = out_weight.shape[0], act_weight.shape[1]
    heads = qkv_cols // (3 * HD) * tensor_size
    bf16, f32 = jnp.bfloat16, jnp.float32
    shape = jax.ShapeDtypeStruct
    tensor_at = lax.axis_index("tensor")
    place = jnp.stack(
        [lax.axis_index("dp"), tensor_at, seq_lengths[0, 0], jnp.int32(own * tensor_size)]
    ).astype(jnp.int32)

    pack1 = jnp.concatenate([qkv_weight, out_weight.T], axis=1)
    gains = jnp.zeros((8, pack1.shape[1]), bf16).at[0, :rows].set(attn_gain).at[1, :rows].set(mlp_gain)
    pieces1 = gather_all(jnp.concatenate([pack1, gains], axis=0))
    edge_l = lax.ppermute(block_in[own - HALF :], "tensor", [(i, i + 1) for i in range(tensor_size - 1)])
    edge_r = lax.ppermute(block_in[:HALF], "tensor", [(i + 1, i) for i in range(tensor_size - 1)])
    pieces2 = gather_all(jnp.concatenate([act_weight, gate_weight, down_weight.T], axis=1))

    period = 6 * HD
    lane = jnp.arange(period)
    freq = THETA ** (-2.0 * (lane % (HD // 2)).astype(f32) / HD)
    spot = tensor_at * own - HALF + jnp.arange(own + 2 * HALF, dtype=jnp.int32)
    spot = spot - jnp.where(spot < seq_lengths[0, 0], 0, seq_lengths[0, 0])
    angle = spot.astype(f32)[:, None] * freq[None, :]
    turning = ((lane // HD) % 3 < 2)[None, :]
    cos_t = jnp.where(turning, jnp.cos(angle), 1.0)
    sin_t = jnp.where(turning, jnp.sin(angle) * jnp.where(lane % HD < HD // 2, -1.0, 1.0)[None, :], 0.0)

    full1, mixed, probs, attended, hidden_res, gain = call(
        functools.partial(attention_kernel, rows),
        "attention",
        13,
        [
            shape((4, width, qkv_cols + head_cols), bf16),
            shape((4, own + 2 * HALF, qkv_cols), bf16),
            shape((heads, own // QROWS, QROWS, QROWS + 2 * HALF), bf16),
            shape((own, width), bf16),
            shape((own, width), f32),
            shape((8, width), f32),
        ],
        [pltpu.VMEM((dp_size, 8, rows), f32)],
        flops=2 * own * width * width * 5,
        moved=12_000_000,
    )(place, edge_l, block_in, edge_r, cos_t, sin_t, *pieces1)

    grad_cols = 3 * units + head_cols
    block_out, grad_res, grad_att, gain2, keep2, send2 = call(
        functools.partial(feed_kernel, rows),
        "feed",
        13,
        [
            shape((own, width), bf16),
            shape((own, width), f32),
            shape((own, width), bf16),
            shape((1, width), f32),
            shape((2 * width, grad_cols), bf16),
            shape((2 * width, grad_cols), bf16),
        ],
        [
            pltpu.VMEM((4, width, 3 * units), bf16),
            pltpu.VMEM((width, own), bf16),
            pltpu.VMEM((width, own), bf16),
            pltpu.VMEM((width, own), bf16),
            pltpu.VMEM((width, own), bf16),
            pltpu.VMEM((width, own), bf16),
        ],
        flops=2 * own * width * units * 4 * 9,
        moved=20_000_000,
    )(place, hidden_res, block_cot, gain, attended, full1, *pieces2)

    own_grads, back_l, back_r = call(
        attention_back_kernel,
        "attention_back",
        6,
        [
            shape((own, 4 * qkv_cols), f32),
            shape((4, HALF, qkv_cols), bf16),
            shape((4, HALF, qkv_cols), bf16),
        ],
        [pltpu.VMEM((own + 2 * HALF, qkv_cols), f32)],
        flops=2 * own * width * width,
        moved=12_000_000,
    )(mixed, probs, attended, grad_att, cos_t, sin_t)
    from_r = lax.ppermute(back_l, "tensor", [(i + 1, i) for i in range(tensor_size - 1)])
    from_l = lax.ppermute(back_r, "tensor", [(i, i + 1) for i in range(tensor_size - 1)])

    total2 = reduce_all(keep2, send2)

    input_grad, keep1, send1 = call(
        functools.partial(finish_kernel, rows),
        "finish",
        8,
        [
            shape((own, width), f32),
            shape((2 * dp_size * (rows + 8), qkv_cols), bf16),
            shape((2 * dp_size * (rows + 8), qkv_cols), bf16),
        ],
        [
            pltpu.VMEM((width, own), bf16),
            pltpu.VMEM((width, own), bf16),
            pltpu.VMEM((dp_size, 8, rows), f32),
        ],
        flops=2 * own * width * width * 6,
        moved=16_000_000,
    )(place, block_in, gain, gain2, grad_res, own_grads, from_l, from_r, full1)
    total1 = reduce_all(keep1, send1)
    return (
        block_out,
        input_grad,
        total1[rows, :rows],
        total1[:rows],
        total2[:, 3 * units :].T,
        total1[rows + 1, :rows],
        total2[:, :units],
        total2[:, units : 2 * units],
        total2[:, 2 * units : 3 * units].T,
    )


def plan_for(mesh):
    dp_size, tensor_size = mesh.shape["dp"], mesh.shape["tensor"]

    def plan(*args):
        rows, own = args[3].shape[0], args[0].shape[0]
        fits = (
            tensor_size == 4
            and dp_size >= 4
            and dp_size & (dp_size - 1) == 0
            and rows % 16 == 0
            and rows <= 128
            and own % QROWS == 0
            and args[1].shape[1] == 1
        )
        return (on_device_tokens if fits else on_device)(*args)

    return plan


def solution(mesh):
    in_specs = (
        P(("dp", "tensor"), None),
        P("dp", None),
        P("dp"),
        P("dp", "tensor"),
        P("tensor", "dp"),
        P("dp"),
        P("dp", "tensor"),
        P("dp", "tensor"),
        P("tensor", "dp"),
        P(("dp", "tensor"), None),
    )
    out_specs = (
        P(("dp", "tensor"), None),
        P(("dp", "tensor"), None),
        P("dp"),
        P("dp", "tensor"),
        P("tensor", "dp"),
        P("dp"),
        P("dp", "tensor"),
        P("dp", "tensor"),
        P("tensor", "dp"),
    )
    return jax.shard_map(
        plan_for(mesh), mesh=mesh, in_specs=in_specs, out_specs=out_specs, check_vma=False
    )
```
